32 devices in a mesh: dp: 16 (over z, y, x), tensor: 2 (over core).
Axes of the slice: x: 2, y: 2, z: 4, core: 2. Of those that a mesh axis runs over, the one named last changes fastest.
Arguments:
- tokens: bfloat16 [4096, 1024], P(('dp', 'tensor')), may hold values from -6 to 6
- cotangent: bfloat16 [4096, 1024], P(('dp', 'tensor')), may hold values from -6 to 6
- lengths: int32 [16], P('dp'), may hold values from 64 to 256, as said below
- w_query: bfloat16 [1024, 2048], P('dp', 'tensor'), may hold values from -0.1875 to 0.1875
- key_matrix: bfloat16 [1024, 1024], P('dp', 'tensor'), may hold values from -0.1875 to 0.1875
- value_matrix: bfloat16 [1024, 1024], P('dp', 'tensor'), may hold values from -0.1875 to 0.1875
- w_out: bfloat16 [1024, 2048], P('dp', 'tensor'), may hold values from -0.375 to 0.375
- w_gate: bfloat16 [1024, 3072], P('dp', 'tensor'), may hold values from -0.1875 to 0.1875
- w_up: bfloat16 [1024, 3072], P('dp', 'tensor'), may hold values from -0.1875 to 0.1875
- w_down: bfloat16 [1024, 3072], P('dp', 'tensor'), may hold values from -0.109375 to 0.109375
- gain_attn: float32 [1024], replicated, may hold values from 0.5 to 2
- gain_mlp: float32 [1024], replicated, may hold values from 0.5 to 2
- gain_query: float32 [128], replicated, may hold values from 0.5 to 2
- gain_key: float32 [128], replicated, may hold values from 0.5 to 2
Outputs:
- result: bfloat16 [4096, 1024], P(('dp', 'tensor'))
- grad_tokens: float32 [4096, 1024], P(('dp', 'tensor'))
- grad_w_query: float32 [1024, 2048], P('dp', 'tensor')
- grad_w_key: float32 [1024, 1024], P('dp', 'tensor')
- grad_w_value: float32 [1024, 1024], P('dp', 'tensor')
- grad_w_out: float32 [1024, 2048], P('dp', 'tensor')
- grad_w_gate: float32 [1024, 3072], P('dp', 'tensor')
- grad_w_up: float32 [1024, 3072], P('dp', 'tensor')
- grad_w_down: float32 [1024, 3072], P('dp', 'tensor')
- grad_gain_attn: float32 [1024], replicated
- grad_gain_mlp: float32 [1024], replicated
- grad_gain_query: float32 [128], replicated
- grad_gain_key: float32 [128], replicated
The draws below stay inside these ranges and needn't reach their ends.
Inputs may be any that keep to these rules, and one draw needn't show every extreme that they name: `lengths`: some sequence fills all 256 token slots of its block.
All inputs are finite; a program needn't handle non-finite values.
Results may differ from the reference program's by a relative error of at most 0.013.
The reference program's roundings to bfloat16 on the way count: a program that leaves them out, or rounds other values in their place, can miss the bound.
Values may be sent and summed in bfloat16 or wider, within the bound.
A program may use at most 128 MiB of HBM per device.

```python
import math
import jax
import jax.numpy as jnp
from jax import lax

MODEL_WIDTH = 1024
QUERY_HEADS = 16
KEY_VALUE_HEADS = 8
HEAD_SIZE = 128
FF = 3072
TOK_DP = 256
TOKENS = 4096
N_DP = 16


def draw_lengths(key, part):
    drawn = jax.random.randint(key, (N_DP,), TOK_DP // 4, TOK_DP + 1, dtype=jnp.int32)
    slots = jnp.arange(N_DP, dtype=jnp.int32)
    drawn = jnp.where(slots == 0, jnp.int32(TOK_DP), drawn)
    drawn = jnp.where(slots == N_DP - 1, jnp.int32(TOK_DP // 4), drawn)
    return drawn.astype(jnp.int32)


def block_levels(key, dims, cuts, smallest, high):
    loudness = 1.0
    for dim, shards_of in cuts:
        heights = jax.random.uniform(jax.random.fold_in(jax.random.fold_in(key, 6), dim), (shards_of,), jnp.float32, smallest / len(cuts), high / len(cuts))
        loudness = loudness * jnp.repeat(jnp.exp(heights), dims[dim] // shards_of).reshape((-1,) + (1,) * (len(dims) - 1 - dim))
    return loudness


def gaussian(key, shape, spread, limit, split=(), kind=jnp.bfloat16):
    array = spread * jax.random.normal(key, shape, jnp.float32)
    if split:
        array = array * block_levels(key, shape, split, -0.22, 0.18)
    return jnp.clip(array, -limit, limit).astype(kind)


def setup_inputs(seed: int = 0) -> dict:
    seeds = jax.random.split(jax.random.key(seed), 15)
    tokens = gaussian(seeds[0], (TOKENS, MODEL_WIDTH), 1.0, 6.0, ((0, 32),))
    cotangent = gaussian(seeds[1], (TOKENS, MODEL_WIDTH), 1.0, 6.0, ((0, 32),))
    lengths = draw_lengths(jax.random.fold_in(seeds[14], 71), 0)
    w_query = gaussian(seeds[3], (MODEL_WIDTH, QUERY_HEADS * HEAD_SIZE), MODEL_WIDTH ** -0.5, 0.1875, ((0, 16), (1, 2)))
    key_matrix = gaussian(seeds[4], (MODEL_WIDTH, KEY_VALUE_HEADS * HEAD_SIZE), MODEL_WIDTH ** -0.5, 0.1875, ((0, 16), (1, 2)))
    value_matrix = gaussian(seeds[5], (MODEL_WIDTH, KEY_VALUE_HEADS * HEAD_SIZE), MODEL_WIDTH ** -0.5, 0.1875, ((0, 16), (1, 2)))
    w_out = gaussian(seeds[6], (MODEL_WIDTH, QUERY_HEADS * HEAD_SIZE), (QUERY_HEADS * HEAD_SIZE // 8) ** -0.5, 0.375, ((0, 16), (1, 2)))
    w_gate = gaussian(seeds[7], (MODEL_WIDTH, FF), MODEL_WIDTH ** -0.5, 0.1875, ((0, 16), (1, 2)))
    w_up = gaussian(seeds[8], (MODEL_WIDTH, FF), MODEL_WIDTH ** -0.5, 0.1875, ((0, 16), (1, 2)))
    w_down = gaussian(seeds[9], (MODEL_WIDTH, FF), FF ** -0.5, 0.109375, ((0, 16), (1, 2)))
    gain_attn = jnp.clip(jnp.exp(jax.random.uniform(seeds[10], (MODEL_WIDTH,), jnp.float32, math.log(0.5), math.log(2.0))), 0.5, 2.0)
    gain_mlp = jnp.clip(jnp.exp(jax.random.uniform(seeds[11], (MODEL_WIDTH,), jnp.float32, math.log(0.5), math.log(2.0))), 0.5, 2.0)
    gain_query = jnp.clip(jnp.exp(jax.random.uniform(seeds[12], (HEAD_SIZE,), jnp.float32, math.log(0.5), math.log(2.0))), 0.5, 2.0)
    gain_key = jnp.clip(jnp.exp(jax.random.uniform(seeds[13], (HEAD_SIZE,), jnp.float32, math.log(0.5), math.log(2.0))), 0.5, 2.0)
    return {"tokens": tokens, "cotangent": cotangent, "lengths": lengths, "w_query": w_query, "key_matrix": key_matrix, "value_matrix": value_matrix, "w_out": w_out, "w_gate": w_gate, "w_up": w_up, "w_down": w_down, "gain_attn": gain_attn, "gain_mlp": gain_mlp, "gain_query": gain_query, "gain_key": gain_key}


norm_eps = 1e-06
rope_base = 1000000.0

def rms_rows(values, gain_vec):
    inverse = lax.rsqrt(lax.optimization_barrier(jnp.mean(values * values, axis=-1, keepdims=True)) + norm_eps)
    return (values * inverse * gain_vec, inverse)

def rms_back(grad_output, values, inverse, gain_vec):
    scaled = grad_output * gain_vec
    mean_term = lax.optimization_barrier(jnp.mean(scaled * values, axis=-1, keepdims=True))
    grad_values = inverse * scaled - values * (inverse * inverse * inverse) * mean_term
    flat_terms = (grad_output * values * inverse).reshape(-1, values.shape[-1])
    return (grad_values, lax.optimization_barrier(jnp.sum(flat_terms, axis=0)))

def layout(length_value, total_rows):
    length_value = jnp.asarray(length_value).astype(jnp.int32)
    indices = jnp.arange(total_rows, dtype=jnp.int32)
    live = indices < length_value
    positions = jnp.where(live, indices, jnp.zeros_like(indices)).astype(jnp.int32)
    causal = live[:, None] & live[None, :] & (indices[None, :] <= indices[:, None])
    allowed = causal | (indices[:, None] == indices[None, :])
    return (positions, allowed, live)

def rope_tables(positions, head_width):
    half_width = head_width // 2
    frequency = jnp.exp(-jnp.log(rope_base) * (2.0 * jnp.arange(half_width, dtype=jnp.float32) / head_width))
    angles = positions.astype(jnp.float32)[:, None] * frequency[None, :]
    return (jnp.cos(angles), jnp.sin(angles))

def rotate(values, cosine, sine_part):
    half_width = values.shape[-1] // 2
    first, second = (values[..., :half_width], values[..., half_width:])
    return jnp.concatenate([first * cosine - second * sine_part, second * cosine + first * sine_part], axis=-1)

def rotate_back(grads, cosine, sine_part):
    half_width = grads.shape[-1] // 2
    first, second = (grads[..., :half_width], grads[..., half_width:])
    return jnp.concatenate([first * cosine + second * sine_part, second * cosine - first * sine_part], axis=-1)

def masked_scores(query_rot, key_rot, allowed, scaling):
    scores = jnp.einsum('qgrd,kgd->grqk', query_rot.astype(jnp.float32), key_rot.astype(jnp.float32)) * scaling
    return jnp.where(allowed, scores, -1e+30)

def layer_group(tokens, cotangent, length_value, params):
    w_query, key_matrix, value_matrix, w_out, w_gate, w_up, w_down, gain_attn, gain_mlp, gain_query, gain_key = params
    total_rows = tokens.shape[0]
    kv_heads = key_matrix.shape[1] // HEAD_SIZE
    group_ratio = w_query.shape[1] // key_matrix.shape[1]
    scaling = HEAD_SIZE ** (-0.5)
    positions, allowed, live = layout(length_value, total_rows)
    cot_live = jnp.where(live[:, None], cotangent, jnp.zeros_like(cotangent))
    cosine, sine_part = rope_tables(positions, HEAD_SIZE)
    cos_query, sin_query = (cosine[:, None, None, :], sine_part[:, None, None, :])
    cos_key, sin_key = (cosine[:, None, :], sine_part[:, None, :])
    token_values = tokens.astype(jnp.float32)
    attn_norm, attn_inverse = rms_rows(token_values, gain_attn)
    normed = attn_norm.astype(jnp.bfloat16)
    query_raw = jnp.dot(normed, w_query, preferred_element_type=jnp.float32).reshape(total_rows, kv_heads, group_ratio, HEAD_SIZE)
    key_raw = jnp.dot(normed, key_matrix, preferred_element_type=jnp.float32).reshape(total_rows, kv_heads, HEAD_SIZE)
    value_part = jnp.dot(normed, value_matrix, preferred_element_type=jnp.float32).astype(jnp.bfloat16).reshape(total_rows, kv_heads, HEAD_SIZE)
    query_normed, query_inverse = rms_rows(query_raw, gain_query)
    key_normed, key_inverse = rms_rows(key_raw, gain_key)
    query_rot = rotate(query_normed, cos_query, sin_query).astype(jnp.bfloat16)
    key_rot = rotate(key_normed, cos_key, sin_key).astype(jnp.bfloat16)
    scores = masked_scores(query_rot, key_rot, allowed, scaling)
    row_max = lax.optimization_barrier(jnp.max(scores, axis=-1, keepdims=True))
    log_total = row_max + jnp.log(lax.optimization_barrier(jnp.sum(jnp.exp(scores - row_max), axis=-1, keepdims=True)))
    attn_probs = jnp.exp(scores - log_total).astype(jnp.bfloat16)
    mixed = jnp.einsum('grqk,kgd->qgrd', attn_probs.astype(jnp.float32), value_part.astype(jnp.float32)).astype(jnp.bfloat16)
    mixed_flat = mixed.reshape(total_rows, -1)
    resid = token_values + jnp.dot(mixed_flat, w_out.T, preferred_element_type=jnp.float32)
    mlp_norm, mlp_inverse = rms_rows(resid, gain_mlp)
    mlp_in = mlp_norm.astype(jnp.bfloat16)
    gate_proj = jnp.dot(mlp_in, w_gate, preferred_element_type=jnp.float32)
    up_proj = jnp.dot(mlp_in, w_up, preferred_element_type=jnp.float32)
    activation = (jax.nn.silu(gate_proj) * up_proj).astype(jnp.bfloat16)
    result = (resid + jnp.dot(activation, w_down.T, preferred_element_type=jnp.float32)).astype(jnp.bfloat16)
    grad_w_down = jnp.dot(cot_live.T, activation, preferred_element_type=jnp.float32)
    grad_act = jnp.dot(cot_live, w_down, preferred_element_type=jnp.float32)
    sigma = jax.nn.sigmoid(gate_proj)
    grad_gate = (grad_act * up_proj * sigma * (1.0 + gate_proj * (1.0 - sigma))).astype(jnp.bfloat16)
    grad_up = (grad_act * gate_proj * sigma).astype(jnp.bfloat16)
    grad_w_gate = jnp.dot(mlp_in.T, grad_gate, preferred_element_type=jnp.float32)
    grad_w_up = jnp.dot(mlp_in.T, grad_up, preferred_element_type=jnp.float32)
    grad_mlp_in = jnp.dot(grad_gate, w_gate.T, preferred_element_type=jnp.float32) + jnp.dot(grad_up, w_up.T, preferred_element_type=jnp.float32)
    grad_resid_mlp, grad_gain_mlp = rms_back(grad_mlp_in, resid, mlp_inverse, gain_mlp)
    grad_resid = cot_live.astype(jnp.float32) + grad_resid_mlp
    grad_attn = grad_resid.astype(jnp.bfloat16)
    grad_w_out = jnp.dot(grad_attn.T, mixed_flat, preferred_element_type=jnp.float32)
    grad_mixed = jnp.dot(grad_attn, w_out, preferred_element_type=jnp.float32).astype(jnp.bfloat16).reshape(total_rows, kv_heads, group_ratio, HEAD_SIZE)
    scores = masked_scores(query_rot, key_rot, allowed, scaling)
    probs_full = jnp.exp(scores - log_total)
    probs_half = probs_full.astype(jnp.bfloat16)
    grad_value = jnp.einsum('grqk,qgrd->kgd', probs_half.astype(jnp.float32), grad_mixed.astype(jnp.float32))
    grad_probs = jnp.einsum('qgrd,kgd->grqk', grad_mixed.astype(jnp.float32), value_part.astype(jnp.float32))
    row_delta = lax.optimization_barrier(jnp.sum(grad_mixed.astype(jnp.float32) * mixed.astype(jnp.float32), axis=-1))
    row_delta = jnp.transpose(row_delta, (1, 2, 0))[..., None]
    grad_scores = (probs_full * (grad_probs - row_delta) * scaling).astype(jnp.bfloat16)
    grad_query_rot = jnp.einsum('grqk,kgd->qgrd', grad_scores.astype(jnp.float32), key_rot.astype(jnp.float32))
    grad_key_rot = jnp.einsum('grqk,qgrd->kgd', grad_scores.astype(jnp.float32), query_rot.astype(jnp.float32))
    grad_query_raw, grad_gain_query = rms_back(rotate_back(grad_query_rot, cos_query, sin_query), query_raw, query_inverse, gain_query)
    grad_key_raw, grad_gain_key = rms_back(rotate_back(grad_key_rot, cos_key, sin_key), key_raw, key_inverse, gain_key)
    grad_query_half = grad_query_raw.astype(jnp.bfloat16).reshape(total_rows, -1)
    grad_key_half = grad_key_raw.astype(jnp.bfloat16).reshape(total_rows, -1)
    grad_value_half = grad_value.astype(jnp.bfloat16).reshape(total_rows, -1)
    grad_w_query = jnp.dot(normed.T, grad_query_half, preferred_element_type=jnp.float32)
    grad_w_key = jnp.dot(normed.T, grad_key_half, preferred_element_type=jnp.float32)
    grad_w_value = jnp.dot(normed.T, grad_value_half, preferred_element_type=jnp.float32)
    grad_normed = jnp.dot(grad_query_half, w_query.T, preferred_element_type=jnp.float32)
    grad_normed = grad_normed + jnp.dot(grad_key_half, key_matrix.T, preferred_element_type=jnp.float32)
    grad_normed = grad_normed + jnp.dot(grad_value_half, value_matrix.T, preferred_element_type=jnp.float32)
    grad_tokens_attn, grad_gain_attn = rms_back(grad_normed, token_values, attn_inverse, gain_attn)
    grad_tokens = grad_resid + grad_tokens_attn
    grads = (grad_w_query, grad_w_key, grad_w_value, grad_w_out, grad_w_gate, grad_w_up, grad_w_down, grad_gain_attn, grad_gain_mlp, grad_gain_query, grad_gain_key)
    return (result, grad_tokens, grads)

def reference(tokens, cotangent, lengths, w_query, key_matrix, value_matrix, w_out, w_gate, w_up, w_down, gain_attn, gain_mlp, gain_query, gain_key):
    params = (w_query, key_matrix, value_matrix, w_out, w_gate, w_up, w_down, gain_attn, gain_mlp, gain_query, gain_key)
    packs = tokens.reshape(N_DP, TOK_DP, MODEL_WIDTH)
    pack_grads = cotangent.reshape(N_DP, TOK_DP, MODEL_WIDTH)
    initial = tuple((jnp.zeros(item.shape, jnp.float32) for item in params))

    def one_pack(carry, item):
        pack_tokens, pack_cotangent, length_value = item
        result, grad_tokens, grads = layer_group(pack_tokens, pack_cotangent, length_value, params)
        summed = tuple((left + right for left, right in zip(carry, grads)))
        return (summed, (result, grad_tokens))
    totals, (results, grad_rows) = lax.scan(one_pack, initial, (packs, pack_grads, lengths.astype(jnp.int32)))
    return (results.reshape(TOKENS, MODEL_WIDTH), grad_rows.reshape(TOKENS, MODEL_WIDTH), totals[0], totals[1], totals[2], totals[3], totals[4], totals[5], totals[6], totals[7], totals[8], totals[9], totals[10])
```

```python
import functools
import math

import jax
import jax.numpy as jnp
from jax import lax
from jax.experimental import pallas as pl
from jax.experimental.pallas import tpu as pltpu
from jax.sharding import PartitionSpec as P

MESH = pl.DeviceIdType.MESH
VMEM_LIMIT = 64000000

QUERY_HEADS = 16
KEY_VALUE_HEADS = 8
HEAD_SIZE = 128


norm_eps = 1e-06
rope_base = 1000000.0


def rms_rows(values, gain_vec):
    inverse = lax.rsqrt(jnp.mean(values * values, axis=-1, keepdims=True) + norm_eps)
    return (values * inverse * gain_vec, inverse)


def rms_back(grad_output, values, inverse, gain_vec):
    scaled = grad_output * gain_vec
    mean_term = jnp.mean(scaled * values, axis=-1, keepdims=True)
    grad_values = inverse * scaled - values * (inverse * inverse * inverse) * mean_term
    flat_terms = (grad_output * values * inverse).reshape(-1, values.shape[-1])
    return (grad_values, jnp.sum(flat_terms, axis=0))


def layout(length_value, total_rows):
    length_value = jnp.asarray(length_value)
    indices = jnp.arange(total_rows, dtype=jnp.int32)
    live = indices < length_value
    positions = jnp.where(live, indices, jnp.zeros_like(indices))
    causal = live[:, None] & live[None, :] & (indices[None, :] <= indices[:, None])
    allowed = causal | (indices[:, None] == indices[None, :])
    return (positions, allowed)


def rope_tables(positions, head_width):
    half_width = head_width // 2
    frequency = jnp.exp(
        -jnp.log(rope_base) * (2.0 * jnp.arange(half_width, dtype=jnp.float32) / head_width)
    )
    angles = positions.astype(jnp.float32)[:, None] * frequency[None, :]
    return (jnp.cos(angles), jnp.sin(angles))


def rotate(values, cosine, sine_part):
    half_width = values.shape[-1] // 2
    first, second = (values[..., :half_width], values[..., half_width:])
    return jnp.concatenate(
        [first * cosine - second * sine_part, second * cosine + first * sine_part], axis=-1
    )


def rotate_back(grads, cosine, sine_part):
    half_width = grads.shape[-1] // 2
    first, second = (grads[..., :half_width], grads[..., half_width:])
    return jnp.concatenate(
        [first * cosine + second * sine_part, second * cosine - first * sine_part], axis=-1
    )


def product_t(left, right):
    return lax.dot_general(
        left, right, (((1,), (1,)), ((), ())), preferred_element_type=jnp.float32
    )


def product_tn(left, right):
    return lax.dot_general(
        left, right, (((0,), (0,)), ((), ())), preferred_element_type=jnp.float32
    )


def split_dims(count):
    sizes, rest = [], count
    for _ in range(2):
        if rest % 2 == 0:
            sizes.append(2)
            rest //= 2
    while rest > 1:
        factor = 4 if rest % 4 == 0 else rest
        sizes.insert(0, factor)
        rest //= factor
    return tuple(sizes)


def dim_orders(sizes):
    k = len(sizes)
    base = list(range(k))
    if k < 2:
        return [tuple(base)]
    swapped = base[:-2] + [base[-1], base[-2]]
    if k < 3:
        return [tuple(base), tuple(swapped)]
    late = [k - 2] + base[: k - 2] + [k - 1]
    late_swapped = [k - 1] + base[: k - 2] + [k - 2]
    return [tuple(base), tuple(swapped), tuple(base), tuple(swapped), tuple(late), tuple(late_swapped)]


def plan_chunks(widths, sizes):
    orders = dim_orders(sizes)
    chunks = []
    for index, width in enumerate(widths):
        parts = 2 if width % 256 == 0 else 1
        for part in range(parts):
            step = width // parts
            chunks.append((index, part * step, step, orders[len(chunks) % len(orders)]))
    return chunks


class Place:
    def __init__(self, sizes):
        self.sizes = sizes
        self.me = lax.axis_index("dp")
        self.strides = [math.prod(sizes[i + 1 :]) for i in range(len(sizes))]
        self.coords = [
            lax.rem(lax.div(self.me, stride), size) for stride, size in zip(self.strides, sizes)
        ]
        self.base = [sum(size - 1 for size in sizes[:i]) for i in range(len(sizes))]

    def other(self, dim, offset):
        return lax.rem(self.coords[dim] + offset, self.sizes[dim])

    def peer(self, dim, offset):
        return self.me + (self.other(dim, offset) - self.coords[dim]) * self.strides[dim]

    def slot(self, dim, offset):
        return self.base[dim] + offset - 1

    def barrier(self, extra=()):
        barrier = pltpu.get_barrier_semaphore()
        count = 0
        for dim, size in enumerate(self.sizes):
            for offset in range(1, size):
                pl.semaphore_signal(
                    barrier, inc=1, device_id={"dp": self.peer(dim, offset)}, device_id_type=MESH
                )
                count += 1
        for target in extra:
            pl.semaphore_signal(barrier, inc=1, device_id=target, device_id_type=MESH)
            count += 1
        pl.semaphore_wait(barrier, count)


def gather_kernel(sizes, chunks, count, *refs):
    ins, outs = refs[:count], refs[count : 2 * count]
    send_sem, recv_sem, local_sem = refs[2 * count :]
    place = Place(sizes)
    k = len(sizes)

    def region(chunk, done, dim=None, coord=None):
        index, start, width, _ = chunk
        where = []
        for i in range(k):
            if i == dim:
                where.append(coord)
            elif i in done:
                where.append(slice(None))
            else:
                where.append(place.coords[i])
        return outs[index].at[tuple(where) + (slice(None), pl.ds(start, width))]

    def sends(j, stage):
        chunk = chunks[j]
        order = chunk[3]
        dim, done = order[stage], order[:stage]
        block = region(chunk, done)
        if stage == 0:
            source = ins[chunk[0]].at[:, pl.ds(chunk[1], chunk[2])]
        else:
            source = block
        return [
            pltpu.make_async_remote_copy(
                src_ref=source,
                dst_ref=block,
                send_sem=send_sem.at[j, place.slot(dim, offset)],
                recv_sem=recv_sem.at[j, place.slot(dim, offset)],
                device_id={"dp": place.peer(dim, offset)},
                device_id_type=MESH,
            )
            for offset in range(1, sizes[dim])
        ]

    def wait_arrivals(j, stage):
        chunk = chunks[j]
        order = chunk[3]
        dim, done = order[stage], order[:stage]
        for offset in range(1, sizes[dim]):
            block = region(chunk, done, dim, place.other(dim, sizes[dim] - offset))
            pltpu.make_async_remote_copy(
                src_ref=block,
                dst_ref=block,
                send_sem=send_sem.at[j, place.slot(dim, offset)],
                recv_sem=recv_sem.at[j, place.slot(dim, offset)],
                device_id={"dp": place.peer(dim, offset)},
                device_id_type=MESH,
            ).wait_recv()

    place.barrier()
    started, own = [], []
    for j, chunk in enumerate(chunks):
        copies = sends(j, 0)
        for copy in copies:
            copy.start()
        started += copies
        copy = pltpu.make_async_copy(
            ins[chunk[0]].at[:, pl.ds(chunk[1], chunk[2])], region(chunk, ()), local_sem.at[j]
        )
        copy.start()
        own.append(copy)
    for step in range(len(chunks) + k - 1):
        for stage in range(1, k + 1):
            j = step - (stage - 1)
            if not 0 <= j < len(chunks):
                continue
            if stage == 1:
                own[j].wait()
            wait_arrivals(j, stage - 1)
            if stage < k:
                copies = sends(j, stage)
                for copy in copies:
                    copy.start()
                started += copies
    for copy in started:
        copy.wait_send()


def gather_weights(weights, collective_id):
    sizes = split_dims(lax.axis_size("dp"))
    chunks = plan_chunks([weight.shape[1] for weight in weights], sizes)
    peers = sum(size - 1 for size in sizes)
    count = len(weights)
    outs = pl.pallas_call(
        functools.partial(gather_kernel, sizes, chunks, count),
        out_shape=[jax.ShapeDtypeStruct(sizes + w.shape, w.dtype) for w in weights],
        in_specs=[pl.BlockSpec(memory_space=pltpu.VMEM)] * count,
        out_specs=[pl.BlockSpec(memory_space=pl.ANY)] * count,
        scratch_shapes=[
            pltpu.SemaphoreType.DMA((len(chunks), peers)),
            pltpu.SemaphoreType.DMA((len(chunks), peers)),
            pltpu.SemaphoreType.DMA((len(chunks),)),
        ],
        compiler_params=pltpu.CompilerParams(
            collective_id=collective_id, has_side_effects=True, vmem_limit_bytes=VMEM_LIMIT
        ),
    )(*weights)
    return [out.reshape(-1, out.shape[-1]) for out in outs]


def reduce_kernel(sizes, chunks, count, tensor_size, *refs):
    ins, gains = refs[:count], refs[count]
    outs, gain_out = refs[count + 1 : 2 * count + 1], refs[2 * count + 1]
    rest = list(refs[2 * count + 2 :])
    k = len(sizes)
    held = [[rest.pop(0) for _ in range(k - 1)] for _ in chunks]
    landed = [[rest.pop(0) for _ in range(k)] for _ in chunks]
    gain_held = [rest.pop(0) for _ in range(k)]
    gain_landed = [rest.pop(0) for _ in range(k + 1)]
    send_sem, recv_sem, local_sem, gain_send, gain_recv = rest
    place = Place(sizes)
    tensor_me = lax.axis_index("tensor")
    rows = ins[0].shape[-2]

    def remote(source, target, send, recv, device):
        return pltpu.make_async_remote_copy(
            src_ref=source,
            dst_ref=target,
            send_sem=send,
            recv_sem=recv,
            device_id=device,
            device_id_type=MESH,
        )

    def part(ref, dims, dim, coord, columns):
        where = tuple(coord if i == dim else slice(None) for i in dims)
        return ref.at[where + (slice(None), columns)]

    def copies_of(j, stage):
        index, start, width, order = chunks[j]
        dim = order[stage]
        dims = [i for i in range(k) if i not in order[:stage]]
        if stage == 0:
            ref, columns = ins[index], pl.ds(start, width)
        else:
            ref, columns = held[j][stage - 1], slice(None)
        result = []
        for offset in range(1, sizes[dim]):
            source = part(ref, dims, dim, place.other(dim, offset), columns)
            slot = place.slot(dim, offset)
            result.append(
                remote(
                    source,
                    landed[j][stage].at[offset - 1],
                    send_sem.at[j, slot],
                    recv_sem.at[j, slot],
                    {"dp": place.peer(dim, offset)},
                )
            )
        return result

    def add_up(j, stage):
        index, start, width, order = chunks[j]
        dim = order[stage]
        dims = [i for i in range(k) if i not in order[:stage]]
        lead = [sizes[i] for i in dims if i != dim]
        blocks = math.prod(lead)
        per = rows // 16

        def body(i, carry):
            rows_at = pl.ds(pl.multiple_of(lax.rem(i, per) * 16, 16), 16)
            flat = lax.div(i, per)
            where = []
            for position in range(len(lead)):
                below = math.prod(lead[position + 1 :])
                where.append(lax.rem(lax.div(flat, below), lead[position]))
            if stage == 0:
                own = tuple(where)
                source = held[j][0]
            else:
                own = list(where)
                own.insert(dims.index(dim), place.coords[dim])
                own = tuple(own)
                source = held[j][stage - 1]
            total = source[own + (rows_at, slice(None))].astype(jnp.float32)
            for offset in range(1, sizes[dim]):
                got = landed[j][stage][(offset - 1,) + tuple(where) + (rows_at, slice(None))]
                total = total + got.astype(jnp.float32)
            if stage < k - 1:
                held[j][stage][tuple(where) + (rows_at, slice(None))] = total.astype(jnp.bfloat16)
            else:
                outs[index][rows_at, pl.ds(start, width)] = total
            return carry

        lax.fori_loop(0, blocks * per, body, 0)

    def gain_copies(stage):
        source = gains if stage == 0 else gain_held[stage - 1]
        result = []
        if stage < k:
            for offset in range(1, sizes[stage]):
                slot = place.slot(stage, offset)
                result.append(
                    remote(
                        source,
                        gain_landed[stage].at[offset - 1],
                        gain_send.at[slot],
                        gain_recv.at[slot],
                        {"dp": place.peer(stage, offset)},
                    )
                )
        else:
            first = sum(size - 1 for size in sizes)
            for offset in range(1, tensor_size):
                result.append(
                    remote(
                        source,
                        gain_landed[stage].at[offset - 1],
                        gain_send.at[first + offset - 1],
                        gain_recv.at[first + offset - 1],
                        {"tensor": lax.rem(tensor_me + offset, tensor_size)},
                    )
                )
        return result

    place.barrier(
        [{"tensor": lax.rem(tensor_me + i, tensor_size)} for i in range(1, tensor_size)]
    )
    flights, own = [], []
    for j, chunk in enumerate(chunks):
        index, start, width, order = chunk
        first = copies_of(j, 0)
        for copy in first:
            copy.start()
        flights.append([first])
        copy = pltpu.make_async_copy(
            part(ins[index], range(k), order[0], place.coords[order[0]], pl.ds(start, width)),
            held[j][0],
            local_sem.at[j],
        )
        copy.start()
        own.append(copy)
        if j == 0:
            gain_flight = gain_copies(0)
            for copy in gain_flight:
                copy.start()
    for step in range(len(chunks) + k - 1):
        if step <= k:
            for copy in gain_flight:
                copy.wait()
            total = (gains if step == 0 else gain_held[step - 1])[...]
            for i in range(len(gain_flight)):
                total = total + gain_landed[step][i]
            if step < k:
                gain_held[step][...] = total
                gain_flight = gain_copies(step + 1)
                for copy in gain_flight:
                    copy.start()
            else:
                gain_out[...] = total
        for stage in range(k):
            j = step - stage
            if not 0 <= j < len(chunks):
                continue
            if stage == 0:
                own[j].wait()
            for copy in flights[j][stage]:
                copy.wait_recv()
            add_up(j, stage)
            if stage < k - 1:
                following = copies_of(j, stage + 1)
                for copy in following:
                    copy.start()
                flights[j].append(following)
    for flight in flights:
        for copies in flight:
            for copy in copies:
                copy.wait_send()


def reduce_weights(grads, gains, collective_id):
    sizes = split_dims(lax.axis_size("dp"))
    tensor_size = lax.axis_size("tensor")
    k = len(sizes)
    dp = math.prod(sizes)
    rows = grads[0].shape[0] // dp
    chunks = [
        (index, start, width, tuple(reversed(order)))
        for index, start, width, order in plan_chunks([g.shape[1] for g in grads], sizes)
    ]
    peers = sum(size - 1 for size in sizes)
    count = len(grads)
    held, landed = [], []
    for _, _, width, order in chunks:
        for stage in range(k):
            left = tuple(sizes[i] for i in range(k) if i not in order[: stage + 1])
            if stage < k - 1:
                held.append(pltpu.VMEM(left + (rows, width), jnp.bfloat16))
            landed.append(pltpu.VMEM((sizes[order[stage]] - 1,) + left + (rows, width), jnp.bfloat16))
    gain_landed = [pltpu.VMEM((size - 1,) + gains.shape, jnp.float32) for size in sizes + (tensor_size,)]
    whole = pl.BlockSpec(memory_space=pltpu.VMEM)
    outs = pl.pallas_call(
        functools.partial(reduce_kernel, sizes, chunks, count, tensor_size),
        out_shape=[jax.ShapeDtypeStruct((rows, g.shape[1]), jnp.float32) for g in grads]
        + [jax.ShapeDtypeStruct(gains.shape, jnp.float32)],
        in_specs=[pl.BlockSpec(memory_space=pl.ANY)] * count + [whole],
        out_specs=[whole] * (count + 1),
        scratch_shapes=held
        + landed
        + [pltpu.VMEM(gains.shape, jnp.float32)] * k
        + gain_landed
        + [
            pltpu.SemaphoreType.DMA((len(chunks), peers)),
            pltpu.SemaphoreType.DMA((len(chunks), peers)),
            pltpu.SemaphoreType.DMA((len(chunks),)),
            pltpu.SemaphoreType.DMA((peers + tensor_size - 1,)),
            pltpu.SemaphoreType.DMA((peers + tensor_size - 1,)),
        ],
        compiler_params=pltpu.CompilerParams(
            collective_id=collective_id, has_side_effects=True, vmem_limit_bytes=VMEM_LIMIT
        ),
    )(*[g.reshape(sizes + (rows, g.shape[1])) for g in grads], gains)
    return outs[:count], outs[count]


def pair_barrier(size):
    me = lax.axis_index("tensor")
    barrier = pltpu.get_barrier_semaphore()
    for offset in range(1, size):
        pl.semaphore_signal(
            barrier, inc=1, device_id={"tensor": lax.rem(me + offset, size)}, device_id_type=MESH
        )
    pl.semaphore_wait(barrier, size - 1)
    return me


def gather_rows_kernel(size, in_ref, out_ref, send_sem, recv_sem):
    me = pair_barrier(size)
    copies = []
    for offset in range(1, size):
        copy = pltpu.make_async_remote_copy(
            src_ref=in_ref,
            dst_ref=out_ref.at[me],
            send_sem=send_sem.at[offset - 1],
            recv_sem=recv_sem.at[offset - 1],
            device_id={"tensor": lax.rem(me + offset, size)},
            device_id_type=MESH,
        )
        copy.start()
        copies.append(copy)
    out_ref[me] = in_ref[...]
    for copy in copies:
        copy.wait()


def gather_rows(values, collective_id):
    size = lax.axis_size("tensor")
    out = pl.pallas_call(
        functools.partial(gather_rows_kernel, size),
        out_shape=jax.ShapeDtypeStruct((size,) + values.shape, values.dtype),
        in_specs=[pl.BlockSpec(memory_space=pltpu.VMEM)],
        out_specs=pl.BlockSpec(memory_space=pltpu.VMEM),
        scratch_shapes=[pltpu.SemaphoreType.DMA((size - 1,))] * 2,
        compiler_params=pltpu.CompilerParams(collective_id=collective_id, has_side_effects=True),
    )(values)
    return out.reshape(-1, values.shape[-1])


def scatter_rows_kernel(size, in_ref, out_ref, landed, send_sem, recv_sem):
    me = pair_barrier(size)
    copies = []
    for offset in range(1, size):
        other = lax.rem(me + offset, size)
        copy = pltpu.make_async_remote_copy(
            src_ref=in_ref.at[other],
            dst_ref=landed.at[offset - 1],
            send_sem=send_sem.at[offset - 1],
            recv_sem=recv_sem.at[offset - 1],
            device_id={"tensor": other},
            device_id_type=MESH,
        )
        copy.start()
        copies.append(copy)
    for copy in copies:
        copy.wait()

    def body(i, carry):
        at = pl.ds(pl.multiple_of(i * 16, 16), 16)
        total = in_ref[me, at, :]
        for offset in range(1, size):
            total = total + landed[offset - 1, at, :]
        out_ref[at, :] = total
        return carry

    lax.fori_loop(0, out_ref.shape[0] // 16, body, 0)


def scatter_rows(partial_sum, collective_id):
    size = lax.axis_size("tensor")
    rows, width = partial_sum.shape[0] // size, partial_sum.shape[1]
    return pl.pallas_call(
        functools.partial(scatter_rows_kernel, size),
        out_shape=jax.ShapeDtypeStruct((rows, width), partial_sum.dtype),
        in_specs=[pl.BlockSpec(memory_space=pltpu.VMEM)],
        out_specs=pl.BlockSpec(memory_space=pltpu.VMEM),
        scratch_shapes=[pltpu.VMEM((size - 1, rows, width), partial_sum.dtype)]
        + [pltpu.SemaphoreType.DMA((size - 1,))] * 2,
        compiler_params=pltpu.CompilerParams(collective_id=collective_id, has_side_effects=True),
    )(partial_sum.reshape(size, rows, width))


def masked_scores(query_rot, key_rot, allowed, scaling):
    scores = (
        jnp.einsum("qgrd,kgd->grqk", query_rot, key_rot, preferred_element_type=jnp.float32)
        * scaling
    )
    return jnp.where(allowed, scores, -1e30)


def per_device(
    tokens,
    cotangent,
    lengths,
    w_query,
    key_matrix,
    value_matrix,
    w_out,
    w_gate,
    w_up,
    w_down,
    gain_attn,
    gain_mlp,
    gain_query,
    gain_key,
):
    own_rows = tokens.shape[0]
    total_rows = own_rows * lax.axis_size("tensor")
    length_value = lengths[0]
    positions, allowed = layout(length_value, total_rows)
    own_index = lax.axis_index("tensor") * own_rows + jnp.arange(own_rows, dtype=jnp.int32)
    own_live = own_index < length_value
    cot_live = jnp.where(own_live[:, None], cotangent, jnp.zeros_like(cotangent))
    cosine, sine_part = rope_tables(positions, HEAD_SIZE)
    cos_query, sin_query = (cosine[:, None, None, :], sine_part[:, None, None, :])
    cos_key, sin_key = (cosine[:, None, :], sine_part[:, None, :])
    scaling = HEAD_SIZE ** (-0.5)
    group_ratio = QUERY_HEADS // KEY_VALUE_HEADS
    token_values = tokens.astype(jnp.float32)
    attn_norm, attn_inverse = rms_rows(token_values, gain_attn)
    normed = gather_rows(attn_norm.astype(jnp.bfloat16), 3)
    fetched = gather_weights(
        (w_query, key_matrix, value_matrix, w_out, w_gate, w_up, w_down), collective_id=0
    )
    full_query, full_key, full_value, full_out, full_gate, full_up, full_down = fetched
    kv_heads = full_key.shape[1] // HEAD_SIZE
    query_raw = jnp.dot(normed, full_query, preferred_element_type=jnp.float32).reshape(
        total_rows, kv_heads, group_ratio, HEAD_SIZE
    )
    key_raw = jnp.dot(normed, full_key, preferred_element_type=jnp.float32).reshape(
        total_rows, kv_heads, HEAD_SIZE
    )
    value_part = (
        jnp.dot(normed, full_value, preferred_element_type=jnp.float32)
        .astype(jnp.bfloat16)
        .reshape(total_rows, kv_heads, HEAD_SIZE)
    )
    query_normed, query_inverse = rms_rows(query_raw, gain_query)
    key_normed, key_inverse = rms_rows(key_raw, gain_key)
    query_rot = rotate(query_normed, cos_query, sin_query).astype(jnp.bfloat16)
    key_rot = rotate(key_normed, cos_key, sin_key).astype(jnp.bfloat16)
    scores = masked_scores(query_rot, key_rot, allowed, scaling)
    row_max = jnp.max(scores, axis=-1, keepdims=True)
    log_total = row_max + jnp.log(jnp.sum(jnp.exp(scores - row_max), axis=-1, keepdims=True))
    attn_probs = jnp.exp(scores - log_total).astype(jnp.bfloat16)
    mixed = jnp.einsum(
        "grqk,kgd->qgrd", attn_probs, value_part, preferred_element_type=jnp.float32
    ).astype(jnp.bfloat16)
    mixed_flat = mixed.reshape(total_rows, -1)
    resid = token_values + scatter_rows(product_t(mixed_flat, full_out), 7)
    mlp_norm, mlp_inverse = rms_rows(resid, gain_mlp)
    mlp_in = gather_rows(mlp_norm.astype(jnp.bfloat16), 4)
    gate_proj = jnp.dot(mlp_in, full_gate, preferred_element_type=jnp.float32)
    up_proj = jnp.dot(mlp_in, full_up, preferred_element_type=jnp.float32)
    activation = (jax.nn.silu(gate_proj) * up_proj).astype(jnp.bfloat16)
    result = (resid + scatter_rows(product_t(activation, full_down), 8)).astype(jnp.bfloat16)
    grad_result = gather_rows(cot_live, 5)
    grad_w_down = product_tn(grad_result, activation)
    grad_act = jnp.dot(grad_result, full_down, preferred_element_type=jnp.float32)
    sigma = jax.nn.sigmoid(gate_proj)
    grad_gate = (grad_act * up_proj * sigma * (1.0 + gate_proj * (1.0 - sigma))).astype(
        jnp.bfloat16
    )
    grad_up = (grad_act * gate_proj * sigma).astype(jnp.bfloat16)
    grad_w_gate = product_tn(mlp_in, grad_gate)
    grad_w_up = product_tn(mlp_in, grad_up)
    grad_mlp_in = scatter_rows(product_t(grad_gate, full_gate) + product_t(grad_up, full_up), 9)
    grad_resid_mlp, grad_gain_mlp = rms_back(grad_mlp_in, resid, mlp_inverse, gain_mlp)
    grad_resid = cot_live.astype(jnp.float32) + grad_resid_mlp
    grad_attn = gather_rows(grad_resid.astype(jnp.bfloat16), 6)
    grad_w_out = product_tn(grad_attn, mixed_flat)
    grad_mixed = (
        jnp.dot(grad_attn, full_out, preferred_element_type=jnp.float32)
        .astype(jnp.bfloat16)
        .reshape(total_rows, kv_heads, group_ratio, HEAD_SIZE)
    )
    scores = masked_scores(query_rot, key_rot, allowed, scaling)
    probs_full = jnp.exp(scores - log_total)
    probs_half = probs_full.astype(jnp.bfloat16)
    grad_value = jnp.einsum(
        "grqk,qgrd->kgd", probs_half, grad_mixed, preferred_element_type=jnp.float32
    )
    grad_probs = jnp.einsum(
        "qgrd,kgd->grqk", grad_mixed, value_part, preferred_element_type=jnp.float32
    )
    row_delta = jnp.sum(grad_mixed.astype(jnp.float32) * mixed.astype(jnp.float32), axis=-1)
    row_delta = jnp.transpose(row_delta, (1, 2, 0))[..., None]
    grad_scores = (probs_full * (grad_probs - row_delta) * scaling).astype(jnp.bfloat16)
    grad_query_rot = jnp.einsum(
        "grqk,kgd->qgrd", grad_scores, key_rot, preferred_element_type=jnp.float32
    )
    grad_key_rot = jnp.einsum(
        "grqk,qgrd->kgd", grad_scores, query_rot, preferred_element_type=jnp.float32
    )
    grad_query_raw, grad_gain_query = rms_back(
        rotate_back(grad_query_rot, cos_query, sin_query), query_raw, query_inverse, gain_query
    )
    grad_key_raw, grad_gain_key = rms_back(
        rotate_back(grad_key_rot, cos_key, sin_key), key_raw, key_inverse, gain_key
    )
    grad_query_half = grad_query_raw.astype(jnp.bfloat16).reshape(total_rows, -1)
    grad_key_half = grad_key_raw.astype(jnp.bfloat16).reshape(total_rows, -1)
    grad_value_half = grad_value.astype(jnp.bfloat16).reshape(total_rows, -1)
    grad_w_query = product_tn(normed, grad_query_half)
    grad_w_key = product_tn(normed, grad_key_half)
    grad_w_value = product_tn(normed, grad_value_half)
    normed_terms = product_t(grad_query_half, full_query) + product_t(grad_key_half, full_key)
    normed_terms = normed_terms + product_t(grad_value_half, full_value)
    grad_normed = scatter_rows(normed_terms, 10)
    grad_tokens_attn, grad_gain_attn = rms_back(grad_normed, token_values, attn_inverse, gain_attn)
    grad_tokens = grad_resid + grad_tokens_attn
    gain_parts = (grad_gain_attn, grad_gain_mlp, grad_gain_query, grad_gain_key)
    gain_rows = [part.reshape(-1, HEAD_SIZE) for part in gain_parts]
    used = sum(part.shape[0] for part in gain_rows)
    gain_rows.append(jnp.zeros((-used % 8, HEAD_SIZE), jnp.float32))
    weight_sums, gain_sum = reduce_weights(
        [
            grad.astype(jnp.bfloat16)
            for grad in (
                grad_w_query,
                grad_w_key,
                grad_w_value,
                grad_w_out,
                grad_w_gate,
                grad_w_up,
                grad_w_down,
            )
        ],
        jnp.concatenate(gain_rows, axis=0),
        collective_id=1,
    )
    gain_totals, row = [], 0
    for part in gain_parts:
        taken = part.shape[0] // HEAD_SIZE
        gain_totals.append(gain_sum[row : row + taken].reshape(-1))
        row += taken
    return (
        result,
        grad_tokens,
        weight_sums[0],
        weight_sums[1],
        weight_sums[2],
        weight_sums[3],
        weight_sums[4],
        weight_sums[5],
        weight_sums[6],
        gain_totals[0],
        gain_totals[1],
        gain_totals[2],
        gain_totals[3],
    )


def solution(mesh):
    in_specs = (
        P(("dp", "tensor"), None),
        P(("dp", "tensor"), None),
        P("dp"),
        P("dp", "tensor"),
        P("dp", "tensor"),
        P("dp", "tensor"),
        P("dp", "tensor"),
        P("dp", "tensor"),
        P("dp", "tensor"),
        P("dp", "tensor"),
        P(),
        P(),
        P(),
        P(),
    )
    out_specs = (
        P(("dp", "tensor"), None),
        P(("dp", "tensor"), None),
        P("dp", "tensor"),
        P("dp", "tensor"),
        P("dp", "tensor"),
        P("dp", "tensor"),
        P("dp", "tensor"),
        P("dp", "tensor"),
        P("dp", "tensor"),
        P(),
        P(),
        P(),
        P(),
    )
    return jax.shard_map(
        per_device, mesh=mesh, in_specs=in_specs, out_specs=out_specs, check_vma=False
    )
```

```python
import functools
import math

import jax
import jax.numpy as jnp
from jax import lax
from jax.experimental import pallas as pl
from jax.experimental.pallas import tpu as pltpu
from jax.sharding import PartitionSpec as P

MESH = pl.DeviceIdType.MESH
VMEM_LIMIT = 64000000

QUERY_HEADS = 16
KEY_VALUE_HEADS = 8
HEAD_SIZE = 128


norm_eps = 1e-06
rope_base = 1000000.0


def rms_rows(values, gain_vec):
    inverse = lax.rsqrt(jnp.mean(values * values, axis=-1, keepdims=True) + norm_eps)
    return (values * inverse * gain_vec, inverse)


def rms_back(grad_output, values, inverse, gain_vec):
    scaled = grad_output * gain_vec
    mean_term = jnp.mean(scaled * values, axis=-1, keepdims=True)
    grad_values = inverse * scaled - values * (inverse * inverse * inverse) * mean_term
    flat_terms = (grad_output * values * inverse).reshape(-1, values.shape[-1])
    return (grad_values, jnp.sum(flat_terms, axis=0))


def layout(length_value, total_rows):
    length_value = jnp.asarray(length_value)
    indices = jnp.arange(total_rows, dtype=jnp.int32)
    live = indices < length_value
    positions = jnp.where(live, indices, jnp.zeros_like(indices))
    causal = live[:, None] & live[None, :] & (indices[None, :] <= indices[:, None])
    allowed = causal | (indices[:, None] == indices[None, :])
    return (positions, allowed)


def rope_tables(positions, head_width):
    half_width = head_width // 2
    frequency = jnp.exp(
        -jnp.log(rope_base) * (2.0 * jnp.arange(half_width, dtype=jnp.float32) / head_width)
    )
    angles = positions.astype(jnp.float32)[:, None] * frequency[None, :]
    return (jnp.cos(angles), jnp.sin(angles))


def rotate(values, cosine, sine_part):
    half_width = values.shape[-1] // 2
    first, second = (values[..., :half_width], values[..., half_width:])
    return jnp.concatenate(
        [first * cosine - second * sine_part, second * cosine + first * sine_part], axis=-1
    )


def rotate_back(grads, cosine, sine_part):
    half_width = grads.shape[-1] // 2
    first, second = (grads[..., :half_width], grads[..., half_width:])
    return jnp.concatenate(
        [first * cosine + second * sine_part, second * cosine - first * sine_part], axis=-1
    )


def product_t(left, right):
    return lax.dot_general(
        left, right, (((1,), (1,)), ((), ())), preferred_element_type=jnp.float32
    )


def product_tn(left, right):
    return lax.dot_general(
        left, right, (((0,), (0,)), ((), ())), preferred_element_type=jnp.float32
    )


def split_dims(count):
    sizes, rest = [], count
    for _ in range(2):
        if rest % 2 == 0:
            sizes.append(2)
            rest //= 2
    while rest > 1:
        factor = 4 if rest % 4 == 0 else rest
        sizes.insert(0, factor)
        rest //= factor
    return tuple(sizes)


def dim_orders(sizes):
    k = len(sizes)
    base = list(range(k))
    if k < 2:
        return [tuple(base)]
    swapped = base[:-2] + [base[-1], base[-2]]
    if k < 3:
        return [tuple(base), tuple(swapped)]
    return [tuple(base), tuple(swapped)]


def plan_chunks(widths, sizes):
    orders = dim_orders(sizes)
    chunks = []
    for index, width in enumerate(widths):
        parts = 2 if width % 256 == 0 else 1
        for part in range(parts):
            step = width // parts
            chunks.append((index, part * step, step, orders[len(chunks) % len(orders)]))
    return chunks


class Place:
    def __init__(self, sizes):
        self.sizes = sizes
        self.me = lax.axis_index("dp")
        self.strides = [math.prod(sizes[i + 1 :]) for i in range(len(sizes))]
        self.coords = [
            lax.rem(lax.div(self.me, stride), size) for stride, size in zip(self.strides, sizes)
        ]
        self.base = [sum(size - 1 for size in sizes[:i]) for i in range(len(sizes))]

    def other(self, dim, offset):
        return lax.rem(self.coords[dim] + offset, self.sizes[dim])

    def peer(self, dim, offset):
        return self.me + (self.other(dim, offset) - self.coords[dim]) * self.strides[dim]

    def slot(self, dim, offset):
        return self.base[dim] + offset - 1

    def barrier(self, extra=()):
        barrier = pltpu.get_barrier_semaphore()
        count = 0
        for dim, size in enumerate(self.sizes):
            for offset in range(1, size):
                pl.semaphore_signal(
                    barrier, inc=1, device_id={"dp": self.peer(dim, offset)}, device_id_type=MESH
                )
                count += 1
        for target in extra:
            pl.semaphore_signal(barrier, inc=1, device_id=target, device_id_type=MESH)
            count += 1
        pl.semaphore_wait(barrier, count)


def gather_kernel(sizes, chunks, count, *refs):
    ins, outs = refs[:count], refs[count : 2 * count]
    send_sem, recv_sem, local_sem = refs[2 * count :]
    place = Place(sizes)
    k = len(sizes)

    def region(chunk, done, dim=None, coord=None):
        index, start, width, _ = chunk
        where = []
        for i in range(k):
            if i == dim:
                where.append(coord)
            elif i in done:
                where.append(slice(None))
            else:
                where.append(place.coords[i])
        return outs[index].at[tuple(where) + (slice(None), pl.ds(start, width))]

    def sends(j, stage):
        chunk = chunks[j]
        order = chunk[3]
        dim, done = order[stage], order[:stage]
        block = region(chunk, done)
        if stage == 0:
            source = ins[chunk[0]].at[:, pl.ds(chunk[1], chunk[2])]
        else:
            source = block
        return [
            pltpu.make_async_remote_copy(
                src_ref=source,
                dst_ref=block,
                send_sem=send_sem.at[j, place.slot(dim, offset)],
                recv_sem=recv_sem.at[j, place.slot(dim, offset)],
                device_id={"dp": place.peer(dim, offset)},
                device_id_type=MESH,
            )
            for offset in range(1, sizes[dim])
        ]

    def wait_arrivals(j, stage):
        chunk = chunks[j]
        order = chunk[3]
        dim, done = order[stage], order[:stage]
        for offset in range(1, sizes[dim]):
            block = region(chunk, done, dim, place.other(dim, sizes[dim] - offset))
            pltpu.make_async_remote_copy(
                src_ref=block,
                dst_ref=block,
                send_sem=send_sem.at[j, place.slot(dim, offset)],
                recv_sem=recv_sem.at[j, place.slot(dim, offset)],
                device_id={"dp": place.peer(dim, offset)},
                device_id_type=MESH,
            ).wait_recv()

    place.barrier()
    started, own = [], []
    for j, chunk in enumerate(chunks):
        copies = sends(j, 0)
        for copy in copies:
            copy.start()
        started += copies
        copy = pltpu.make_async_copy(
            ins[chunk[0]].at[:, pl.ds(chunk[1], chunk[2])], region(chunk, ()), local_sem.at[j]
        )
        copy.start()
        own.append(copy)
    for step in range(len(chunks) + k - 1):
        for stage in range(1, k + 1):
            j = step - (stage - 1)
            if not 0 <= j < len(chunks):
                continue
            if stage == 1:
                own[j].wait()
            wait_arrivals(j, stage - 1)
            if stage < k:
                copies = sends(j, stage)
                for copy in copies:
                    copy.start()
                started += copies
    for copy in started:
        copy.wait_send()


def gather_weights(weights, collective_id):
    sizes = split_dims(lax.axis_size("dp"))
    chunks = plan_chunks([weight.shape[1] for weight in weights], sizes)
    peers = sum(size - 1 for size in sizes)
    count = len(weights)
    outs = pl.pallas_call(
        functools.partial(gather_kernel, sizes, chunks, count),
        out_shape=[jax.ShapeDtypeStruct(sizes + w.shape, w.dtype) for w in weights],
        in_specs=[pl.BlockSpec(memory_space=pltpu.VMEM)] * count,
        out_specs=[pl.BlockSpec(memory_space=pl.ANY)] * count,
        scratch_shapes=[
            pltpu.SemaphoreType.DMA((len(chunks), peers)),
            pltpu.SemaphoreType.DMA((len(chunks), peers)),
            pltpu.SemaphoreType.DMA((len(chunks),)),
        ],
        compiler_params=pltpu.CompilerParams(
            collective_id=collective_id, has_side_effects=True, vmem_limit_bytes=VMEM_LIMIT
        ),
    )(*weights)
    return [out.reshape(-1, out.shape[-1]) for out in outs]


def reduce_kernel(sizes, chunks, count, tensor_size, *refs):
    ins, gains = refs[:count], refs[count]
    outs, gain_out = refs[count + 1 : 2 * count + 1], refs[2 * count + 1]
    rest = list(refs[2 * count + 2 :])
    k = len(sizes)
    held = [[rest.pop(0) for _ in range(k - 1)] for _ in chunks]
    landed = [[rest.pop(0) for _ in range(k)] for _ in chunks]
    gain_held = [rest.pop(0) for _ in range(k)]
    gain_landed = [rest.pop(0) for _ in range(k + 1)]
    send_sem, recv_sem, local_sem, gain_send, gain_recv = rest
    place = Place(sizes)
    tensor_me = lax.axis_index("tensor")
    rows = ins[0].shape[-2]

    def remote(source, target, send, recv, device):
        return pltpu.make_async_remote_copy(
            src_ref=source,
            dst_ref=target,
            send_sem=send,
            recv_sem=recv,
            device_id=device,
            device_id_type=MESH,
        )

    def part(ref, dims, dim, coord, columns):
        where = tuple(coord if i == dim else slice(None) for i in dims)
        return ref.at[where + (slice(None), columns)]

    def copies_of(j, stage):
        index, start, width, order = chunks[j]
        dim = order[stage]
        dims = [i for i in range(k) if i not in order[:stage]]
        if stage == 0:
            ref, columns = ins[index], pl.ds(start, width)
        else:
            ref, columns = held[j][stage - 1], slice(None)
        result = []
        for offset in range(1, sizes[dim]):
            source = part(ref, dims, dim, place.other(dim, offset), columns)
            slot = place.slot(dim, offset)
            result.append(
                remote(
                    source,
                    landed[j][stage].at[offset - 1],
                    send_sem.at[j, slot],
                    recv_sem.at[j, slot],
                    {"dp": place.peer(dim, offset)},
                )
            )
        return result

    def add_up(j, stage):
        index, start, width, order = chunks[j]
        dim = order[stage]
        dims = [i for i in range(k) if i not in order[:stage]]
        lead = [sizes[i] for i in dims if i != dim]
        blocks = math.prod(lead)
        per = rows // 16

        def body(i, carry):
            rows_at = pl.ds(pl.multiple_of(lax.rem(i, per) * 16, 16), 16)
            flat = lax.div(i, per)
            where = []
            for position in range(len(lead)):
                below = math.prod(lead[position + 1 :])
                where.append(lax.rem(lax.div(flat, below), lead[position]))
            if stage == 0:
                own = tuple(where)
                source = held[j][0]
            else:
                own = list(where)
                own.insert(dims.index(dim), place.coords[dim])
                own = tuple(own)
                source = held[j][stage - 1]
            total = source[own + (rows_at, slice(None))].astype(jnp.float32)
            for offset in range(1, sizes[dim]):
                got = landed[j][stage][(offset - 1,) + tuple(where) + (rows_at, slice(None))]
                total = total + got.astype(jnp.float32)
            if stage < k - 1:
                held[j][stage][tuple(where) + (rows_at, slice(None))] = total.astype(jnp.bfloat16)
            else:
                outs[index][rows_at, pl.ds(start, width)] = total
            return carry

        lax.fori_loop(0, blocks * per, body, 0)

    def gain_copies(stage):
        source = gains if stage == 0 else gain_held[stage - 1]
        result = []
        if stage < k:
            for offset in range(1, sizes[stage]):
                slot = place.slot(stage, offset)
                result.append(
                    remote(
                        source,
                        gain_landed[stage].at[offset - 1],
                        gain_send.at[slot],
                        gain_recv.at[slot],
                        {"dp": place.peer(stage, offset)},
                    )
                )
        else:
            first = sum(size - 1 for size in sizes)
            for offset in range(1, tensor_size):
                result.append(
                    remote(
                        source,
                        gain_landed[stage].at[offset - 1],
                        gain_send.at[first + offset - 1],
                        gain_recv.at[first + offset - 1],
                        {"tensor": lax.rem(tensor_me + offset, tensor_size)},
                    )
                )
        return result

    place.barrier(
        [{"tensor": lax.rem(tensor_me + i, tensor_size)} for i in range(1, tensor_size)]
    )
    flights, own = [], []
    for j, chunk in enumerate(chunks):
        index, start, width, order = chunk
        first = copies_of(j, 0)
        for copy in first:
            copy.start()
        flights.append([first])
        copy = pltpu.make_async_copy(
            part(ins[index], range(k), order[0], place.coords[order[0]], pl.ds(start, width)),
            held[j][0],
            local_sem.at[j],
        )
        copy.start()
        own.append(copy)
        if j == 0:
            gain_flight = gain_copies(0)
            for copy in gain_flight:
                copy.start()
    for step in range(len(chunks) + k - 1):
        if step <= k:
            for copy in gain_flight:
                copy.wait()
            total = (gains if step == 0 else gain_held[step - 1])[...]
            for i in range(len(gain_flight)):
                total = total + gain_landed[step][i]
            if step < k:
                gain_held[step][...] = total
                gain_flight = gain_copies(step + 1)
                for copy in gain_flight:
                    copy.start()
            else:
                gain_out[...] = total
        for stage in range(k):
            j = step - stage
            if not 0 <= j < len(chunks):
                continue
            if stage == 0:
                own[j].wait()
            for copy in flights[j][stage]:
                copy.wait_recv()
            add_up(j, stage)
            if stage < k - 1:
                following = copies_of(j, stage + 1)
                for copy in following:
                    copy.start()
                flights[j].append(following)
    for flight in flights:
        for copies in flight:
            for copy in copies:
                copy.wait_send()


def reduce_weights(grads, gains, collective_id):
    sizes = split_dims(lax.axis_size("dp"))
    tensor_size = lax.axis_size("tensor")
    k = len(sizes)
    dp = math.prod(sizes)
    rows = grads[0].shape[0] // dp
    chunks = [
        (index, start, width, tuple(reversed(order)))
        for index, start, width, order in plan_chunks([g.shape[1] for g in grads], sizes)
    ]
    peers = sum(size - 1 for size in sizes)
    count = len(grads)
    held, landed = [], []
    for _, _, width, order in chunks:
        for stage in range(k):
            left = tuple(sizes[i] for i in range(k) if i not in order[: stage + 1])
            if stage < k - 1:
                held.append(pltpu.VMEM(left + (rows, width), jnp.bfloat16))
            landed.append(pltpu.VMEM((sizes[order[stage]] - 1,) + left + (rows, width), jnp.bfloat16))
    gain_landed = [pltpu.VMEM((size - 1,) + gains.shape, jnp.float32) for size in sizes + (tensor_size,)]
    whole = pl.BlockSpec(memory_space=pltpu.VMEM)
    outs = pl.pallas_call(
        functools.partial(reduce_kernel, sizes, chunks, count, tensor_size),
        out_shape=[jax.ShapeDtypeStruct((rows, g.shape[1]), jnp.float32) for g in grads]
        + [jax.ShapeDtypeStruct(gains.shape, jnp.float32)],
        in_specs=[pl.BlockSpec(memory_space=pl.ANY)] * count + [whole],
        out_specs=[whole] * (count + 1),
        scratch_shapes=held
        + landed
        + [pltpu.VMEM(gains.shape, jnp.float32)] * k
        + gain_landed
        + [
            pltpu.SemaphoreType.DMA((len(chunks), peers)),
            pltpu.SemaphoreType.DMA((len(chunks), peers)),
            pltpu.SemaphoreType.DMA((len(chunks),)),
            pltpu.SemaphoreType.DMA((peers + tensor_size - 1,)),
            pltpu.SemaphoreType.DMA((peers + tensor_size - 1,)),
        ],
        compiler_params=pltpu.CompilerParams(
            collective_id=collective_id, has_side_effects=True, vmem_limit_bytes=VMEM_LIMIT
        ),
    )(*[g.reshape(sizes + (rows, g.shape[1])) for g in grads], gains)
    return outs[:count], outs[count]


def pair_barrier(size):
    me = lax.axis_index("tensor")
    barrier = pltpu.get_barrier_semaphore()
    for offset in range(1, size):
        pl.semaphore_signal(
            barrier, inc=1, device_id={"tensor": lax.rem(me + offset, size)}, device_id_type=MESH
        )
    pl.semaphore_wait(barrier, size - 1)
    return me


def gather_rows_kernel(size, in_ref, out_ref, send_sem, recv_sem):
    me = pair_barrier(size)
    copies = []
    for offset in range(1, size):
        copy = pltpu.make_async_remote_copy(
            src_ref=in_ref,
            dst_ref=out_ref.at[me],
            send_sem=send_sem.at[offset - 1],
            recv_sem=recv_sem.at[offset - 1],
            device_id={"tensor": lax.rem(me + offset, size)},
            device_id_type=MESH,
        )
        copy.start()
        copies.append(copy)
    out_ref[me] = in_ref[...]
    for copy in copies:
        copy.wait()


def gather_rows(values, collective_id):
    size = lax.axis_size("tensor")
    out = pl.pallas_call(
        functools.partial(gather_rows_kernel, size),
        out_shape=jax.ShapeDtypeStruct((size,) + values.shape, values.dtype),
        in_specs=[pl.BlockSpec(memory_space=pltpu.VMEM)],
        out_specs=pl.BlockSpec(memory_space=pltpu.VMEM),
        scratch_shapes=[pltpu.SemaphoreType.DMA((size - 1,))] * 2,
        compiler_params=pltpu.CompilerParams(collective_id=collective_id, has_side_effects=True),
    )(values)
    return out.reshape(-1, values.shape[-1])


def scatter_rows_kernel(size, in_ref, out_ref, landed, send_sem, recv_sem):
    me = pair_barrier(size)
    copies = []
    for offset in range(1, size):
        other = lax.rem(me + offset, size)
        copy = pltpu.make_async_remote_copy(
            src_ref=in_ref.at[other],
            dst_ref=landed.at[offset - 1],
            send_sem=send_sem.at[offset - 1],
            recv_sem=recv_sem.at[offset - 1],
            device_id={"tensor": other},
            device_id_type=MESH,
        )
        copy.start()
        copies.append(copy)
    for copy in copies:
        copy.wait()

    def body(i, carry):
        at = pl.ds(pl.multiple_of(i * 16, 16), 16)
        total = in_ref[me, at, :]
        for offset in range(1, size):
            total = total + landed[offset - 1, at, :]
        out_ref[at, :] = total
        return carry

    lax.fori_loop(0, out_ref.shape[0] // 16, body, 0)


def scatter_rows(partial_sum, collective_id):
    size = lax.axis_size("tensor")
    rows, width = partial_sum.shape[0] // size, partial_sum.shape[1]
    return pl.pallas_call(
        functools.partial(scatter_rows_kernel, size),
        out_shape=jax.ShapeDtypeStruct((rows, width), partial_sum.dtype),
        in_specs=[pl.BlockSpec(memory_space=pltpu.VMEM)],
        out_specs=pl.BlockSpec(memory_space=pltpu.VMEM),
        scratch_shapes=[pltpu.VMEM((size - 1, rows, width), partial_sum.dtype)]
        + [pltpu.SemaphoreType.DMA((size - 1,))] * 2,
        compiler_params=pltpu.CompilerParams(collective_id=collective_id, has_side_effects=True),
    )(partial_sum.reshape(size, rows, width))


def masked_scores(query_rot, key_rot, allowed, scaling):
    scores = (
        jnp.einsum("qgrd,kgd->grqk", query_rot, key_rot, preferred_element_type=jnp.float32)
        * scaling
    )
    return jnp.where(allowed, scores, -1e30)


def per_device(
    tokens,
    cotangent,
    lengths,
    w_query,
    key_matrix,
    value_matrix,
    w_out,
    w_gate,
    w_up,
    w_down,
    gain_attn,
    gain_mlp,
    gain_query,
    gain_key,
):
    own_rows = tokens.shape[0]
    total_rows = own_rows * lax.axis_size("tensor")
    length_value = lengths[0]
    positions, allowed = layout(length_value, total_rows)
    own_index = lax.axis_index("tensor") * own_rows + jnp.arange(own_rows, dtype=jnp.int32)
    own_live = own_index < length_value
    cot_live = jnp.where(own_live[:, None], cotangent, jnp.zeros_like(cotangent))
    cosine, sine_part = rope_tables(positions, HEAD_SIZE)
    cos_query, sin_query = (cosine[:, None, None, :], sine_part[:, None, None, :])
    cos_key, sin_key = (cosine[:, None, :], sine_part[:, None, :])
    scaling = HEAD_SIZE ** (-0.5)
    group_ratio = QUERY_HEADS // KEY_VALUE_HEADS
    token_values = tokens.astype(jnp.float32)
    attn_norm, attn_inverse = rms_rows(token_values, gain_attn)
    normed = gather_rows(attn_norm.astype(jnp.bfloat16), 3)
    full_up = lax.all_gather(w_up, "dp", axis=0, tiled=True)
    full_down = lax.all_gather(w_down, "dp", axis=0, tiled=True)
    fetched = gather_weights(
        (w_query, key_matrix, value_matrix, w_out, w_gate), collective_id=0
    )
    full_query, full_key, full_value, full_out, full_gate = fetched
    kv_heads = full_key.shape[1] // HEAD_SIZE
    query_raw = jnp.dot(normed, full_query, preferred_element_type=jnp.float32).reshape(
        total_rows, kv_heads, group_ratio, HEAD_SIZE
    )
    key_raw = jnp.dot(normed, full_key, preferred_element_type=jnp.float32).reshape(
        total_rows, kv_heads, HEAD_SIZE
    )
    value_part = (
        jnp.dot(normed, full_value, preferred_element_type=jnp.float32)
        .astype(jnp.bfloat16)
        .reshape(total_rows, kv_heads, HEAD_SIZE)
    )
    query_normed, query_inverse = rms_rows(query_raw, gain_query)
    key_normed, key_inverse = rms_rows(key_raw, gain_key)
    query_rot = rotate(query_normed, cos_query, sin_query).astype(jnp.bfloat16)
    key_rot = rotate(key_normed, cos_key, sin_key).astype(jnp.bfloat16)
    scores = masked_scores(query_rot, key_rot, allowed, scaling)
    row_max = jnp.max(scores, axis=-1, keepdims=True)
    log_total = row_max + jnp.log(jnp.sum(jnp.exp(scores - row_max), axis=-1, keepdims=True))
    attn_probs = jnp.exp(scores - log_total).astype(jnp.bfloat16)
    mixed = jnp.einsum(
        "grqk,kgd->qgrd", attn_probs, value_part, preferred_element_type=jnp.float32
    ).astype(jnp.bfloat16)
    mixed_flat = mixed.reshape(total_rows, -1)
    resid = token_values + scatter_rows(product_t(mixed_flat, full_out), 7)
    mlp_norm, mlp_inverse = rms_rows(resid, gain_mlp)
    mlp_in = gather_rows(mlp_norm.astype(jnp.bfloat16), 4)
    gate_proj = jnp.dot(mlp_in, full_gate, preferred_element_type=jnp.float32)
    up_proj = jnp.dot(mlp_in, full_up, preferred_element_type=jnp.float32)
    activation = (jax.nn.silu(gate_proj) * up_proj).astype(jnp.bfloat16)
    result = (resid + scatter_rows(product_t(activation, full_down), 8)).astype(jnp.bfloat16)
    grad_result = gather_rows(cot_live, 5)
    grad_w_down = product_tn(grad_result, activation)
    grad_act = jnp.dot(grad_result, full_down, preferred_element_type=jnp.float32)
    sigma = jax.nn.sigmoid(gate_proj)
    grad_gate = (grad_act * up_proj * sigma * (1.0 + gate_proj * (1.0 - sigma))).astype(
        jnp.bfloat16
    )
    grad_up = (grad_act * gate_proj * sigma).astype(jnp.bfloat16)
    grad_w_gate = product_tn(mlp_in, grad_gate)
    grad_w_up = product_tn(mlp_in, grad_up)
    grad_mlp_in = scatter_rows(product_t(grad_gate, full_gate) + product_t(grad_up, full_up), 9)
    grad_resid_mlp, grad_gain_mlp = rms_back(grad_mlp_in, resid, mlp_inverse, gain_mlp)
    grad_resid = cot_live.astype(jnp.float32) + grad_resid_mlp
    grad_attn = gather_rows(grad_resid.astype(jnp.bfloat16), 6)
    grad_w_out = product_tn(grad_attn, mixed_flat)
    grad_mixed = (
        jnp.dot(grad_attn, full_out, preferred_element_type=jnp.float32)
        .astype(jnp.bfloat16)
        .reshape(total_rows, kv_heads, group_ratio, HEAD_SIZE)
    )
    scores = masked_scores(query_rot, key_rot, allowed, scaling)
    probs_full = jnp.exp(scores - log_total)
    probs_half = probs_full.astype(jnp.bfloat16)
    grad_value = jnp.einsum(
        "grqk,qgrd->kgd", probs_half, grad_mixed, preferred_element_type=jnp.float32
    )
    grad_probs = jnp.einsum(
        "qgrd,kgd->grqk", grad_mixed, value_part, preferred_element_type=jnp.float32
    )
    row_delta = jnp.sum(grad_mixed.astype(jnp.float32) * mixed.astype(jnp.float32), axis=-1)
    row_delta = jnp.transpose(row_delta, (1, 2, 0))[..., None]
    grad_scores = (probs_full * (grad_probs - row_delta) * scaling).astype(jnp.bfloat16)
    grad_query_rot = jnp.einsum(
        "grqk,kgd->qgrd", grad_scores, key_rot, preferred_element_type=jnp.float32
    )
    grad_key_rot = jnp.einsum(
        "grqk,qgrd->kgd", grad_scores, query_rot, preferred_element_type=jnp.float32
    )
    grad_query_raw, grad_gain_query = rms_back(
        rotate_back(grad_query_rot, cos_query, sin_query), query_raw, query_inverse, gain_query
    )
    grad_key_raw, grad_gain_key = rms_back(
        rotate_back(grad_key_rot, cos_key, sin_key), key_raw, key_inverse, gain_key
    )
    grad_query_half = grad_query_raw.astype(jnp.bfloat16).reshape(total_rows, -1)
    grad_key_half = grad_key_raw.astype(jnp.bfloat16).reshape(total_rows, -1)
    grad_value_half = grad_value.astype(jnp.bfloat16).reshape(total_rows, -1)
    grad_w_query = product_tn(normed, grad_query_half)
    grad_w_key = product_tn(normed, grad_key_half)
    grad_w_value = product_tn(normed, grad_value_half)
    normed_terms = product_t(grad_query_half, full_query) + product_t(grad_key_half, full_key)
    normed_terms = normed_terms + product_t(grad_value_half, full_value)
    grad_normed = scatter_rows(normed_terms, 10)
    grad_tokens_attn, grad_gain_attn = rms_back(grad_normed, token_values, attn_inverse, gain_attn)
    grad_tokens = grad_resid + grad_tokens_attn
    gain_parts = (grad_gain_attn, grad_gain_mlp, grad_gain_query, grad_gain_key)
    gain_rows = [part.reshape(-1, HEAD_SIZE) for part in gain_parts]
    used = sum(part.shape[0] for part in gain_rows)
    gain_rows.append(jnp.zeros((-used % 8, HEAD_SIZE), jnp.float32))
    weight_sums, gain_sum = reduce_weights(
        [
            grad.astype(jnp.bfloat16)
            for grad in (
                grad_w_query,
                grad_w_key,
                grad_w_value,
                grad_w_out,
                grad_w_gate,
                grad_w_up,
            )
        ],
        jnp.concatenate(gain_rows, axis=0),
        collective_id=1,
    )
    gain_totals, row = [], 0
    for part in gain_parts:
        taken = part.shape[0] // HEAD_SIZE
        gain_totals.append(gain_sum[row : row + taken].reshape(-1))
        row += taken
    down_sum = lax.psum_scatter(grad_w_down, "dp", scatter_dimension=0, tiled=True)
    return (
        result,
        grad_tokens,
        weight_sums[0],
        weight_sums[1],
        weight_sums[2],
        weight_sums[3],
        weight_sums[4],
        weight_sums[5],
        down_sum,
        gain_totals[0],
        gain_totals[1],
        gain_totals[2],
        gain_totals[3],
    )


def solution(mesh):
    in_specs = (
        P(("dp", "tensor"), None),
        P(("dp", "tensor"), None),
        P("dp"),
        P("dp", "tensor"),
        P("dp", "tensor"),
        P("dp", "tensor"),
        P("dp", "tensor"),
        P("dp", "tensor"),
        P("dp", "tensor"),
        P("dp", "tensor"),
        P(),
        P(),
        P(),
        P(),
    )
    out_specs = (
        P(("dp", "tensor"), None),
        P(("dp", "tensor"), None),
        P("dp", "tensor"),
        P("dp", "tensor"),
        P("dp", "tensor"),
        P("dp", "tensor"),
        P("dp", "tensor"),
        P("dp", "tensor"),
        P("dp", "tensor"),
        P(),
        P(),
        P(),
        P(),
    )
    return jax.shard_map(
        per_device, mesh=mesh, in_specs=in_specs, out_specs=out_specs, check_vma=False
    )
```
